32 devices in a mesh: groups: 2 (over y), tmpl: 16 (over z, x, core).
Axes of the slice: x: 2, y: 2, z: 4, core: 2. Of those that a mesh axis runs over, the one named last changes fastest.
Arguments:
- records: bfloat16 [512, 3, 768], P(('groups', 'tmpl')), parts along dimension 0, may hold values from -200 to 200, as said below
- templates: bfloat16 [96, 20, 3, 300], P('tmpl'), may hold values from -6 to 6
- fetch_list: int32 [16, 16, 2], P('tmpl'), may hold values from -1 to 15, as said below
- cluster_slots: int32 [96, 20], P('tmpl'), may hold values from 0 to 31, as said below
- moveouts: int32 [96, 20], P('tmpl'), may hold values from 0 to 213
Outputs:
- stack: float32 [192, 256], P(('groups', 'tmpl')), parts along dimension 0
- network_peak: float32 [512], P('groups'), parts along dimension 0
The draws below stay inside these ranges and needn't reach their ends.
There are 2 independent parts, one for each index of `groups`. The reference program is written for one: setup_inputs(seed, part) draws one part's arguments, and reference() takes and returns one part's arrays. A program takes and returns all parts, laid end to end along the dimension named above; an argument that names none is the same for every part. Nothing has to cross between parts.
Inputs may be any that keep to these rules, and one draw needn't show every extreme that they name: Values are the records' samples; the amplitude of a station component is steady apart from one event burst. fetch_list[g, o, s] is an index among holder o's 16 stations, or -1 for an empty slot; the set entries of one (g, o) pair differ; every group g has all 2 slots set for the holders g to g + 20 // 2 - 1 (modulo 16). cluster_slots[k, j] is a slot o * 2 + s of group k // 6 whose fetch_list entry is set; the 20 entries of a station set differ, and every set slot of a group is named by some station set of that group.
All inputs are finite; a program needn't handle non-finite values.
Results may differ from the reference program's by a relative error of at most 0.0003.
Values may be sent and summed in bfloat16 or wider, within the bound.
A program may use at most 64 MiB of HBM per device.

```python
import math
import jax
import jax.numpy as jnp
from jax import lax

NSTAT = 20
TAPS = 300
OUT = 256
STA_DEV = 16
CAP = 2
CLUST = 6
TPC = 1
REC = 768
MOVE = 214
OWNERS = 16
STATIONS = 256
TEMPLATES = 96


def draw_plan(key):
    seed_key = jax.random.fold_in(key, 4051)
    key_rank, key_count, key_pick, key_shuffle = jax.random.split(seed_key, 4)
    owners = OWNERS
    slot_count = OWNERS * CAP
    group_ids = jnp.arange(owners, dtype=jnp.int32)[:, None, None]
    owner_ids = jnp.arange(owners, dtype=jnp.int32)[None, :, None]
    distance = (owner_ids - group_ids) % owners
    forced = jnp.broadcast_to(distance < NSTAT // CAP, (owners, owners, CAP)).reshape(owners, slot_count)
    column = jnp.arange(slot_count, dtype=jnp.int32)[None, :]
    spread = 2 ** 18
    scores = jax.random.randint(key_rank, (owners, slot_count), 0, spread) * slot_count + column + forced.astype(jnp.int32) * (spread * slot_count)
    ranking = jnp.argsort(-scores, axis=1)
    placing = jnp.argsort(ranking, axis=1)
    lowest = max(NSTAT, slot_count * 2 // 5)
    highest = min(CLUST * NSTAT, slot_count)
    live_count = jax.random.randint(key_count, (owners, 1), lowest, highest + 1)
    filled = placing < live_count
    keyed = jax.random.randint(key_pick, (owners, owners, STA_DEV), 0, spread) * STA_DEV + jnp.arange(STA_DEV, dtype=jnp.int32)
    picked = jnp.argsort(keyed, axis=2)[:, :, :CAP].astype(jnp.int32)
    fetch_ids = jnp.where(filled.reshape(owners, owners, CAP), picked, -1).astype(jnp.int32)
    shuffle = jnp.where(filled, jax.random.randint(key_shuffle, (owners, slot_count), 0, spread) * slot_count + column, spread * slot_count + column)
    listed = jnp.argsort(shuffle, axis=1).astype(jnp.int32)
    position = (jnp.arange(CLUST, dtype=jnp.int32)[:, None] * NSTAT + jnp.arange(NSTAT, dtype=jnp.int32)[None, :]).reshape(1, CLUST * NSTAT) % live_count
    chosen = jnp.take_along_axis(listed, position, axis=1)
    return (fetch_ids, chosen.reshape(owners * CLUST, NSTAT).astype(jnp.int32))


def draw_fetch_list(key, part):
    fetch_ids, chosen = draw_plan(key)
    return fetch_ids


def draw_cluster_slots(key, part):
    fetch_ids, chosen = draw_plan(key)
    return chosen


def draw_records(key, part):
    key_noise, key_scale, key_centre, key_width = jax.random.split(jax.random.fold_in(key, 911), 4)
    shape = (STATIONS, 3, REC)
    noise = jax.random.truncated_normal(key_noise, -5.0, 5.0, shape, jnp.float32)
    amplitude = jnp.exp(jax.random.uniform(key_scale, (STATIONS, 3, 1), jnp.float32, 0.0, math.log(10.0)))
    centre = jax.random.uniform(key_centre, (STATIONS, 1, 1), jnp.float32, 0.0, REC)
    breadth = jax.random.uniform(key_width, (STATIONS, 1, 1), jnp.float32, REC / 32.0, REC / 8.0)
    times = jnp.arange(REC, dtype=jnp.float32)[None, None, :]
    envelope = 1.0 + 3.0 * jnp.exp(-((times - centre) / breadth) ** 2)
    return (noise * amplitude * envelope).astype(jnp.bfloat16)


def plant(result, key, smallest, largest):
    shape = result.shape
    spot = [jax.random.randint(jax.random.fold_in(key, axis), (), 0, shape[axis]) for axis in range(len(shape))]
    result = result.at[tuple(spot)].set(smallest)
    longest = shape.index(max(shape))
    spot[longest] = (spot[longest] + 1) % shape[longest]
    return result.at[tuple(spot)].set(largest)


def level_of(rng, shape, shards, least, high):
    def one(dim, blocks):
        heights = jax.random.uniform(jax.random.fold_in(jax.random.fold_in(rng, 6), dim), (blocks,), jnp.float32, least / len(shards), high / len(shards))
        return jnp.repeat(jnp.exp(heights), shape[dim] // blocks).reshape((-1,) + (1,) * (len(shape) - dim - 1))

    level = one(*shards[0])
    for cut in shards[1:]:
        level = level * one(*cut)
    return level


def centred(rng, dims, scale, reach, pieces=(), kind=jnp.bfloat16):
    gain = level_of(rng, dims, pieces, -0.22, 0.18) if pieces else 1.0
    result = jax.random.normal(rng, dims, jnp.float32) * scale * gain
    return jnp.minimum(jnp.maximum(result, -reach), reach).astype(kind)


def setup_inputs(seed: int = 0, part: int = 0) -> dict:
    splits = jax.random.split(jax.random.key(seed), 6)
    part_keys = jax.random.split(jax.random.fold_in(splits[5], part), 6)
    records = draw_records(jax.random.fold_in(jax.random.fold_in(splits[5], part), 71), part)
    templates = centred(splits[1], (TEMPLATES, NSTAT, 3, TAPS), 1.0, 6.0, ((0, 16),))
    fetch_list = draw_fetch_list(jax.random.fold_in(splits[5], 71), part)
    cluster_slots = draw_cluster_slots(jax.random.fold_in(splits[5], 71), part)
    moveouts = plant(jax.random.randint(splits[4], (TEMPLATES, NSTAT), 0, MOVE), jax.random.fold_in(splits[4], 1), 0, MOVE - 1).astype(jnp.int32)
    return {"records": records, "templates": templates, "fetch_list": fetch_list, "cluster_slots": cluster_slots, "moveouts": moveouts}


def align_row(series, offset):
    return lax.dynamic_slice_in_dim(series, offset.astype(jnp.int32), OUT)

def cluster_stack(traces, kernels, shifts):
    tap_count = kernels.shape[-1]
    members = kernels.shape[0]
    stations = traces.shape[0]
    inputs_nch = traces.reshape(1, stations * 3, traces.shape[-1])
    filters = jnp.transpose(kernels, (1, 2, 0, 3)).reshape(stations * 3 * members, 1, tap_count)
    products = lax.conv_general_dilated(inputs_nch, filters, (1,), 'VALID', dimension_numbers=('NCH', 'OIH', 'NCH'), feature_group_count=stations * 3, precision=lax.Precision.HIGHEST, preferred_element_type=jnp.float32)[0]
    lag_count = products.shape[-1]
    products = products.reshape(stations, 3, members, lag_count)
    energy = lax.reduce_window(traces * traces, jnp.array(0, traces.dtype), lax.add, (1, 1, tap_count), (1, 1, 1), 'VALID')
    data_scale = jnp.sqrt(energy / tap_count + 1e-05)
    tmpl_scale = jnp.sqrt(lax.optimization_barrier(jnp.mean(kernels * kernels, axis=-1)) + 1e-05)
    normed = products / (tap_count * jnp.transpose(tmpl_scale, (1, 2, 0))[..., None] * data_scale[:, :, None, :])
    channel_sum = lax.optimization_barrier(jnp.sum(normed, axis=1))
    aligned = jax.vmap(jax.vmap(align_row))(channel_sum, shifts.T)
    return lax.optimization_barrier(jnp.sum(aligned, axis=0))

def reference(records, templates, fetch_list, cluster_slots, moveouts):
    clusters = cluster_slots.shape[0]
    group_ids = jnp.arange(clusters, dtype=jnp.int32) // CLUST
    owner_ids = cluster_slots // CAP
    within = cluster_slots % CAP
    local_ids = fetch_list[group_ids[:, None], owner_ids, within]
    station_ids = (owner_ids * STA_DEV + local_ids).astype(jnp.int32)
    kernels_all = templates.reshape(clusters, TPC, NSTAT, 3, TAPS)
    shifts_all = moveouts.reshape(clusters, TPC, NSTAT)

    def one_cluster(inputs):
        ids, kernels, shifts = inputs
        traces = jnp.take(records, ids, axis=0).astype(jnp.float32)
        return cluster_stack(traces, kernels.astype(jnp.float32), shifts)
    stacks = lax.map(one_cluster, (station_ids, kernels_all, shifts_all))
    stack = stacks.reshape(clusters * TPC, OUT)
    return (stack, lax.optimization_barrier(jnp.max(stack, axis=0)))
```

```python
import functools

import jax
import jax.numpy as jnp
from jax import lax
from jax.experimental import pallas as pl
from jax.experimental.pallas import tpu as pltpu
from jax.sharding import PartitionSpec as P

OUT = 256
LANES = 128
VMEM = pltpu.VMEM
SMEM = pltpu.SMEM


def greet_all(n, me):
    barrier = pltpu.get_barrier_semaphore()

    def greet(d, carry):
        pl.semaphore_signal(
            barrier,
            inc=1,
            device_id={"tmpl": lax.rem(me + d, n)},
            device_id_type=pl.DeviceIdType.MESH,
        )
        return carry

    lax.fori_loop(1, n, greet, 0)
    pl.semaphore_wait(barrier, n - 1)


def push(src, dst, send, recv, peer):
    return pltpu.make_async_remote_copy(
        src_ref=src,
        dst_ref=dst,
        send_sem=send,
        recv_sem=recv,
        device_id={"tmpl": peer},
        device_id_type=pl.DeviceIdType.MESH,
    )


def fetch_kernel(n, stations, list_ref, rec_ref, out_ref, req_ref, asked, stage, s1, r1, s2, r2):
    me = lax.axis_index("tmpl")
    row = lax.broadcasted_iota(jnp.int32, (8, LANES), 0)
    comp = lax.rem(row, 4)

    def request(o, carry):
        wanted = jnp.where(row < 4, list_ref[0, o], list_ref[1, o])
        valid = jnp.logical_and(wanted >= 0, comp < 3)
        req_ref[o] = jnp.where(valid, comp * stations + wanted, -1)
        return carry

    lax.fori_loop(0, n, request, 0)
    greet_all(n, me)

    def ask(d):
        peer = lax.rem(me + d, n)
        return push(req_ref.at[peer], asked.at[me], s1.at[d], r1.at[d], peer)

    def give(d):
        peer = lax.rem(me + d, n)
        return push(stage.at[peer], out_ref.at[me], s2.at[d], r2.at[d], peer)

    def each(action):
        def body(d, carry):
            action(d)
            return carry

        lax.fori_loop(1, n, body, 0)

    each(lambda d: ask(d).start())
    asked[me] = req_ref[me]
    each(lambda d: ask(d).wait())
    rows = n * 8
    depth = rec_ref.shape[0]
    want = asked[...].reshape(rows, LANES)[:, :depth]
    lane = lax.broadcasted_iota(jnp.int32, (rows, depth), 1)
    onehot = jnp.where(want == lane, 1.0, 0.0).astype(jnp.bfloat16)
    picked = jnp.dot(onehot, rec_ref[...], preferred_element_type=jnp.float32)
    stage[...] = picked.reshape(n, 8, picked.shape[-1]).astype(jnp.bfloat16)
    each(lambda d: give(d).start())
    out_ref[me] = stage[me]
    each(lambda d: give(d).wait())


def fetch(wanted, rec_flat, stations):
    n = wanted.shape[1]
    width = rec_flat.shape[-1]
    return pl.pallas_call(
        functools.partial(fetch_kernel, n, stations),
        out_shape=jax.ShapeDtypeStruct((n, 8, width), jnp.bfloat16),
        in_specs=[pl.BlockSpec(memory_space=SMEM), pl.BlockSpec(memory_space=VMEM)],
        out_specs=pl.BlockSpec(memory_space=VMEM),
        scratch_shapes=[
            pltpu.VMEM((n, 8, LANES), jnp.int32),
            pltpu.VMEM((n, 8, LANES), jnp.int32),
            pltpu.VMEM((n, 8, width), jnp.bfloat16),
            pltpu.SemaphoreType.DMA((n,)),
            pltpu.SemaphoreType.DMA((n,)),
            pltpu.SemaphoreType.DMA((n,)),
            pltpu.SemaphoreType.DMA((n,)),
        ],
        compiler_params=pltpu.CompilerParams(collective_id=0, has_side_effects=True),
        name="fetch_rows",
    )(wanted, rec_flat)


def stack_kernel(
    taps, sets, nstat, slots_ref, moves_ref, rx_ref, tm_ref, stack_ref, peak_ref, comb, rolled, xt, hs, ht_ref
):
    n, _, width = rx_ref.shape
    pairs = sets * nstat
    row = lax.broadcasted_iota(jnp.int32, (8, width), 0)

    def ahead(v, k):
        return pltpu.roll(v, width - k, 1)

    def scale_owner(o, carry):
        x = rx_ref[o].astype(jnp.float32)
        run = x * x
        total = None
        done = 0
        size = 1
        pieces = []
        while size <= taps:
            if taps & size:
                pieces.append((size, run))
            size *= 2
            if size <= taps:
                run = run + ahead(run, size // 2)
        for size, piece in reversed(pieces):
            shifted = ahead(piece, done) if done else piece
            total = shifted if total is None else total + shifted
            done += size
        inv = lax.rsqrt(total / taps + 1e-05)
        first = jnp.where(row < 4, x, pltpu.roll(inv, 4, 0))
        second = jnp.where(row < 4, pltpu.roll(x, 4, 0), inv)
        comb[2 * o, :, :width] = first
        comb[2 * o + 1, :, :width] = second
        return carry

    lax.fori_loop(0, n, scale_owner, 0)

    used = xt.shape[1] // LANES
    lane = lax.broadcasted_iota(jnp.int32, (8, LANES), 1)

    def align_set(k, carry):
        for j in range(nstat):
            slot = slots_ref[k, j]
            move = moves_ref[k, j]
            base = move // LANES
            rest = move - base * LANES
            shift = (LANES - rest) & (LANES - 1)
            start = pl.multiple_of(base * LANES, LANES)
            keep = lane < LANES - rest
            tile = comb[slot, :, pl.ds(start, (used + 1) * LANES)]
            turned = [
                pltpu.roll(tile[:, v * LANES : (v + 1) * LANES], shift, 1) for v in range(used + 1)
            ]
            for v in range(used):
                rolled[k * nstat + j, :, v * LANES : (v + 1) * LANES] = jnp.where(
                    keep, turned[v], turned[v + 1]
                )
        return carry

    lax.fori_loop(0, sets, align_set, 0)

    for c in range(3):
        for v in range(used):
            block = rolled[:, c, v * LANES : (v + 1) * LANES]
            xt[c, v * LANES : (v + 1) * LANES, :] = block.T

    for c in range(3):
        for k in range(sets):
            hs[c, k * nstat : (k + 1) * nstat, :taps] = tm_ref[k, c].astype(jnp.float32)
        for v in range(ht_ref.shape[1] // LANES):
            ht_ref[c, v * LANES : (v + 1) * LANES, :] = hs[c, :, v * LANES : (v + 1) * LANES].T

    chans = []
    half = 128
    for t0 in range(0, OUT, half):
        chan = jnp.zeros((half, LANES), jnp.float32)
        for c in range(3):
            h = ht_ref[c, :taps, :]
            tscale = jnp.sqrt(jnp.sum(h * h, axis=0, keepdims=True) / taps + 1e-05)

            def tap_step(i, acc):
                for f in range(6):
                    tap = i * 6 + f
                    acc = acc + ht_ref[c, pl.ds(tap, 1), :] * xt[c, pl.ds(t0 + tap, half), :]
                return acc

            cc = lax.fori_loop(0, taps // 6, tap_step, jnp.zeros((half, LANES), jnp.float32))
            inv = rolled[:, 4 + c, t0 : t0 + half].T
            chan = chan + cc * (1.0 / (taps * tscale)) * inv
        chans.append(chan.T)
    whole = jnp.concatenate(chans, axis=1)
    rows = [
        jnp.sum(whole[k * nstat : (k + 1) * nstat], axis=0, keepdims=True) for k in range(sets)
    ]
    stack = jnp.concatenate(rows, axis=0)
    stack_ref[...] = stack
    peak_ref[...] = jnp.max(stack, axis=0, keepdims=True)


def local_stack(slots, moves, rx, kernels):
    taps = kernels.shape[-1]
    padded = -(-taps // LANES) * LANES
    n, _, width = rx.shape
    sets, nstat = slots.shape
    used = -(-(OUT + taps - 1) // LANES)
    return pl.pallas_call(
        functools.partial(stack_kernel, taps, sets, nstat),
        out_shape=(
            jax.ShapeDtypeStruct((sets, OUT), jnp.float32),
            jax.ShapeDtypeStruct((1, OUT), jnp.float32),
        ),
        in_specs=[
            pl.BlockSpec(memory_space=SMEM),
            pl.BlockSpec(memory_space=SMEM),
            pl.BlockSpec(memory_space=VMEM),
            pl.BlockSpec(memory_space=VMEM),
        ],
        out_specs=(pl.BlockSpec(memory_space=VMEM), pl.BlockSpec(memory_space=VMEM)),
        scratch_shapes=[
            pltpu.VMEM((2 * n, 8, width + LANES), jnp.float32),
            pltpu.VMEM((LANES, 8, used * LANES), jnp.float32),
            pltpu.VMEM((3, used * LANES, LANES), jnp.float32),
            pltpu.VMEM((3, LANES, padded), jnp.float32),
            pltpu.VMEM((3, padded, LANES), jnp.float32),
        ],
        compiler_params=pltpu.CompilerParams(vmem_limit_bytes=40 << 20),
        name="local_stack",
    )(slots, moves, rx, kernels)


def peak_kernel(n, peak_ref, out_ref, held, send, recv):
    me = lax.axis_index("tmpl")
    greet_all(n, me)

    def copy(d):
        peer = lax.rem(me + d, n)
        return push(peak_ref, held.at[me], send.at[d], recv.at[d], peer)

    def start(d, carry):
        copy(d).start()
        return carry

    def wait(d, carry):
        copy(d).wait()
        return carry

    lax.fori_loop(1, n, start, 0)
    held[me] = peak_ref[...]
    lax.fori_loop(1, n, wait, 0)
    out_ref[...] = jnp.max(held[...], axis=0)


def peak_all(peak, n):
    return pl.pallas_call(
        functools.partial(peak_kernel, n),
        out_shape=jax.ShapeDtypeStruct(peak.shape, jnp.float32),
        in_specs=[pl.BlockSpec(memory_space=VMEM)],
        out_specs=pl.BlockSpec(memory_space=VMEM),
        scratch_shapes=[
            pltpu.VMEM((n,) + peak.shape, jnp.float32),
            pltpu.SemaphoreType.DMA((n,)),
            pltpu.SemaphoreType.DMA((n,)),
        ],
        compiler_params=pltpu.CompilerParams(collective_id=1, has_side_effects=True),
        name="peak_all",
    )(peak)


def on_device(records, templates, fetch_list, cluster_slots, moveouts):
    n = fetch_list.shape[1]
    stations, comps, width = records.shape
    rec_flat = jnp.transpose(records, (1, 0, 2)).reshape(comps * stations, width)
    rx = fetch(jnp.transpose(fetch_list[0]), rec_flat, stations)
    kernels = jnp.transpose(templates, (0, 2, 1, 3))
    stack, peak = local_stack(cluster_slots, moveouts, rx, kernels)
    return stack, peak_all(peak, n).reshape(OUT)


def solution(mesh):
    placed = (
        P(("groups", "tmpl"), None, None),
        P("tmpl", None, None, None),
        P("tmpl", None, None),
        P("tmpl", None),
        P("tmpl", None),
    )
    return jax.shard_map(
        on_device,
        mesh=mesh,
        in_specs=placed,
        out_specs=(P(("groups", "tmpl"), None), P("groups")),
        check_vma=False,
    )
```

```python
import functools

import jax
import jax.numpy as jnp
from jax import lax
from jax.experimental import pallas as pl
from jax.experimental.pallas import tpu as pltpu
from jax.sharding import PartitionSpec as P

OUT = 256
LANES = 128


def push(src, dst, send, recv, peer):
    return pltpu.make_async_remote_copy(
        src_ref=src,
        dst_ref=dst,
        send_sem=send,
        recv_sem=recv,
        device_id={"tmpl": peer},
        device_id_type=pl.DeviceIdType.MESH,
    )


def each(low, high, action):
    def body(d, carry):
        action(d)
        return carry

    lax.fori_loop(low, high, body, 0)


def kernel(
    n, stations, sets, nstat, taps,
    list_ref, slots_ref, moves_ref, rec_hbm, tm_hbm,
    stack_ref, peak_ref,
    rec_ref, tm_ref, req_ref, asked, stage, rx_ref, ids, xs, ys, es, xt, it, hs, ht, tinv, chan, mine, held,
    local, s1, r1, s2, r2, s3, r3,
):
    me = lax.axis_index("tmpl")
    tm_copy = pltpu.make_async_copy(tm_hbm, tm_ref, local.at[0])
    rec_copy = pltpu.make_async_copy(rec_hbm, rec_ref, local.at[1])
    tm_copy.start()
    rec_copy.start()

    barrier = pltpu.get_barrier_semaphore()
    each(1, n, lambda d: pl.semaphore_signal(
        barrier, inc=1, device_id={"tmpl": lax.rem(me + d, n)},
        device_id_type=pl.DeviceIdType.MESH))

    row = lax.broadcasted_iota(jnp.int32, (8, LANES), 0)
    comp = lax.rem(row, 4)

    def request(o):
        wanted = jnp.where(row < 4, list_ref[0, o], list_ref[1, o])
        valid = jnp.logical_and(wanted >= 0, comp < 3)
        req_ref[o] = jnp.where(valid, comp * stations + wanted, -1)

    each(0, n, request)
    pl.semaphore_wait(barrier, n - 1)

    def ask(d):
        peer = lax.rem(me + d, n)
        return push(req_ref.at[peer], asked.at[me], s1.at[d], r1.at[d], peer)

    def give(d):
        peer = lax.rem(me + d, n)
        return push(stage.at[peer], rx_ref.at[me], s2.at[d], r2.at[d], peer)

    def tell(d):
        peer = lax.rem(me + d, n)
        return push(mine, held.at[me], s3.at[d], r3.at[d], peer)

    each(1, n, lambda d: ask(d).start())
    ids[0:8, :] = jnp.full((8, LANES), -1, jnp.int32)
    ids[8:16, :] = jnp.zeros((8, LANES), jnp.int32)
    for k in range(sets):
        ids[0:1, k * nstat : (k + 1) * nstat] = slots_ref[k : k + 1, :]
        ids[8:9, k * nstat : (k + 1) * nstat] = moves_ref[k : k + 1, :]
    asked[me] = req_ref[me]

    tm_copy.wait()
    for c in range(3):
        for k in range(sets):
            hs[c, k * nstat : (k + 1) * nstat, :taps] = tm_ref[k, c].astype(jnp.float32)
        for v in range(ht.shape[1] // LANES):
            ht[c, v * LANES : (v + 1) * LANES, :] = hs[c, :, v * LANES : (v + 1) * LANES].T
        h = ht[c, :taps, :]
        tscale = jnp.sqrt(jnp.sum(h * h, axis=0, keepdims=True) / taps + 1e-05)
        tinv[c] = jnp.broadcast_to(1.0 / (taps * tscale), (8, LANES))

    rec_copy.wait()
    each(1, n, lambda d: ask(d).wait())
    rows = n * 8
    depth, width = rec_ref.shape
    want = asked[...].reshape(rows, LANES)[:, :depth]
    spot = lax.broadcasted_iota(jnp.int32, (rows, depth), 1)
    onehot = jnp.where(want == spot, 1.0, 0.0).astype(jnp.bfloat16)
    picked = jnp.dot(onehot, rec_ref[...], preferred_element_type=jnp.float32)
    stage[...] = picked.reshape(n, 8, width).astype(jnp.bfloat16)
    each(1, n, lambda d: give(d).start())
    rx_ref[me] = stage[me]

    each(1, n, lambda d: give(d).wait())

    spot = lax.broadcasted_iota(jnp.int32, (rows, LANES), 0)
    slot = ids[0:1, :] * 4
    chosen = jnp.concatenate(
        [jnp.where(spot == slot + c, 1.0, 0.0) for c in range(3)], axis=1
    ).astype(jnp.bfloat16)
    got = rx_ref[...].reshape(rows, width)
    picked = lax.dot_general(
        got, chosen, (((0,), (0,)), ((), ())), preferred_element_type=jnp.float32
    )
    for c in range(3):
        xs[c, :width, :] = picked[:, c * LANES : (c + 1) * LANES]

    moves = jnp.broadcast_to(ids[8:9, :], (8, LANES))
    bits = {b: (moves & b) != 0 for b in (128, 64, 32, 16, 8, 4, 2, 1)}

    def choose(bit, one, zero):
        return [jnp.where(bits[bit], p, q) for p, q in zip(one, zero)]

    def coarse(c, b):
        at = b * 64
        tiles = [xs[c, pl.ds(at + 8 * q, 8), :] for q in range(39)]
        for bit in (128, 64, 32, 16, 8):
            tiles = choose(bit, tiles[bit // 8 :], tiles[: -(bit // 8)])
        for q, tile in enumerate(tiles):
            ys[pl.ds(at + 8 * q, 8), :] = tile

    def fine(c, b):
        for q in range(5):
            at = b * 40 + 8 * q
            tiles = [ys[pl.ds(at + i, 8), :] for i in range(8)]
            for bit in (4, 2, 1):
                tiles = choose(bit, tiles[bit : 2 * bit], tiles[:bit])
            xt[c, pl.ds(at, 8), :] = tiles[0]

    def squares(c, at, count):
        total = None
        for i in range(count):
            x = xt[c, pl.ds(at + i, 8), :]
            total = x * x if total is None else total + x * x
        return total

    def eights(c, b):
        for q in range(4):
            at = b * 32 + 8 * q
            es[pl.ds(at, 8), :] = squares(c, at, 8)

    steps = taps // 8
    rest = taps - steps * 8

    def scales(c):
        run = [es[8 * q : 8 * q + 8, :] for q in range(OUT // 8 + steps - 1)]
        pieces = []
        size = 1
        while size <= steps:
            if steps & size:
                pieces.append((size, run))
            run = [p + q for p, q in zip(run, run[size:])]
            size *= 2
        for q in range(OUT // 8):
            done = 0
            total = squares(c, 8 * (q + steps), rest) if rest else None
            for size, piece in reversed(pieces):
                term = piece[q + done]
                total = term if total is None else total + term
                done += size
            it[c, 8 * q : 8 * q + 8, :] = lax.rsqrt(total / taps + 1e-05) * tinv[c]

    chan[...] = jnp.zeros_like(chan)
    tiles = 16
    span = tiles * 8

    def component(c):
        each(0, 9, lambda b: coarse(c, b))
        each(0, 14, lambda b: fine(c, b))
        each(0, 17, lambda b: eights(c, b))
        scales(c)
        for t0 in range(0, OUT, span):

            def phase(f, acc):
                win = [xt[c, pl.ds(t0 + f + 8 * q, 8), :] for q in range(tiles)]
                for e in range(steps):
                    h = jnp.broadcast_to(ht[c, pl.ds(f + 8 * e, 1), :], (8, LANES))
                    acc = tuple(a + h * w for a, w in zip(acc, win))
                    if e < steps - 1:
                        win = win[1:] + [xt[c, pl.ds(t0 + f + 8 * (tiles + e), 8), :]]
                return acc

            acc = tuple(jnp.zeros((8, LANES), jnp.float32) for _ in range(tiles))
            acc = lax.fori_loop(0, 8, phase, acc)
            for tap in range(taps // 8 * 8, taps):
                h = jnp.broadcast_to(ht[c, pl.ds(tap, 1), :], (8, LANES))
                acc = tuple(
                    a + h * xt[c, pl.ds(t0 + tap + 8 * q, 8), :] for q, a in enumerate(acc)
                )
            for q in range(tiles):
                at = pl.ds(t0 + 8 * q, 8)
                chan[at, :] += acc[q] * it[c, at, :]

    each(0, 3, component)
    flat = jnp.concatenate([chan[v : v + LANES].T for v in range(0, OUT, LANES)], axis=1)
    stack = jnp.concatenate(
        [jnp.sum(flat[k * nstat : (k + 1) * nstat], axis=0, keepdims=True) for k in range(sets)],
        axis=0,
    )
    stack_ref[...] = stack
    best = jnp.max(stack, axis=0, keepdims=True)
    mine[...] = best
    each(1, n, lambda d: tell(d).start())
    held[me] = best
    each(1, n, lambda d: tell(d).wait())
    peak_ref[...] = jnp.max(held[...], axis=0)


def on_device(records, templates, fetch_list, cluster_slots, moveouts):
    n = fetch_list.shape[1]
    stations, comps, width = records.shape
    sets, nstat = cluster_slots.shape
    taps = templates.shape[-1]
    padded = -(-taps // LANES) * LANES
    used = -(-(OUT + taps - 1) // LANES)
    rec_flat = jnp.transpose(records, (1, 0, 2)).reshape(comps * stations, width)
    kernels = jnp.transpose(templates, (0, 2, 1, 3))
    vmem = pl.BlockSpec(memory_space=pltpu.VMEM)
    smem = pl.BlockSpec(memory_space=pltpu.SMEM)
    far = pl.BlockSpec(memory_space=pltpu.HBM)
    sems = pltpu.SemaphoreType.DMA((n,))
    stack, peak = pl.pallas_call(
        functools.partial(kernel, n, stations, sets, nstat, taps),
        out_shape=(
            jax.ShapeDtypeStruct((sets, OUT), jnp.float32),
            jax.ShapeDtypeStruct((1, OUT), jnp.float32),
        ),
        in_specs=[smem, vmem, vmem, far, far],
        out_specs=(vmem, vmem),
        scratch_shapes=[
            pltpu.VMEM(rec_flat.shape, jnp.bfloat16),
            pltpu.VMEM(kernels.shape, jnp.bfloat16),
            pltpu.VMEM((n, 8, LANES), jnp.int32),
            pltpu.VMEM((n, 8, LANES), jnp.int32),
            pltpu.VMEM((n, 8, width), jnp.bfloat16),
            pltpu.VMEM((n, 8, width), jnp.bfloat16),
            pltpu.VMEM((16, LANES), jnp.int32),
            pltpu.VMEM((3, 832, LANES), jnp.float32),
            pltpu.VMEM((576, LANES), jnp.float32),
            pltpu.VMEM((544, LANES), jnp.float32),
            pltpu.VMEM((3, used * LANES, LANES), jnp.float32),
            pltpu.VMEM((3, OUT, LANES), jnp.float32),
            pltpu.VMEM((3, LANES, padded), jnp.float32),
            pltpu.VMEM((3, padded, LANES), jnp.float32),
            pltpu.VMEM((3, 8, LANES), jnp.float32),
            pltpu.VMEM((OUT, LANES), jnp.float32),
            pltpu.VMEM((1, OUT), jnp.float32),
            pltpu.VMEM((n, 1, OUT), jnp.float32),
            pltpu.SemaphoreType.DMA((2,)),
            sems, sems, sems, sems, sems, sems,
        ],
        compiler_params=pltpu.CompilerParams(
            collective_id=0, has_side_effects=True, vmem_limit_bytes=40 << 20
        ),
        name="network_stack",
    )(jnp.transpose(fetch_list[0]), cluster_slots, moveouts, rec_flat, kernels)
    return stack, peak.reshape(OUT)


def solution(mesh):
    placed = (
        P(("groups", "tmpl"), None, None),
        P("tmpl", None, None, None),
        P("tmpl", None, None),
        P("tmpl", None),
        P("tmpl", None),
    )
    return jax.shard_map(
        on_device,
        mesh=mesh,
        in_specs=placed,
        out_specs=(P(("groups", "tmpl"), None), P("groups")),
        check_vma=False,
    )
```

```python
import functools

import jax
import jax.numpy as jnp
from jax import lax
from jax.experimental import pallas as pl
from jax.experimental.pallas import tpu as pltpu
from jax.sharding import PartitionSpec as P

OUT = 256
LANES = 128


def push(src, dst, send, recv, peer):
    return pltpu.make_async_remote_copy(
        src_ref=src,
        dst_ref=dst,
        send_sem=send,
        recv_sem=recv,
        device_id={"tmpl": peer},
        device_id_type=pl.DeviceIdType.MESH,
    )


def each(low, high, action):
    def body(d, carry):
        action(d)
        return carry

    lax.fori_loop(low, high, body, 0)


def kernel(
    n, stations, sets, nstat, taps,
    list_hbm, slots_hbm, moves_hbm, rec_hbm, tm_hbm,
    stack_ref, peak_ref,
    list_ref, slots_ref, moves_ref, rec_ref, tm_ref, req_ref, asked, stage, rx_ref, ids, xs, ys, es, xt, it, hs, ht, tinv, chan, mine, held,
    local, s1, r1, s2, r2, s3, r3,
):
    me = lax.axis_index("tmpl")
    tm_copy = pltpu.make_async_copy(tm_hbm, tm_ref, local.at[0])
    rec_copy = pltpu.make_async_copy(rec_hbm, rec_ref, local.at[1])
    list_copy = pltpu.make_async_copy(list_hbm, list_ref, local.at[2])
    slots_copy = pltpu.make_async_copy(slots_hbm, slots_ref, local.at[3])
    moves_copy = pltpu.make_async_copy(moves_hbm, moves_ref, local.at[4])
    list_copy.start()
    rec_copy.start()
    slots_copy.start()
    moves_copy.start()
    tm_copy.start()

    barrier = pltpu.get_barrier_semaphore()
    each(1, n, lambda d: pl.semaphore_signal(
        barrier, inc=1, device_id={"tmpl": lax.rem(me + d, n)},
        device_id_type=pl.DeviceIdType.MESH))

    row = lax.broadcasted_iota(jnp.int32, (8, LANES), 0)
    comp = lax.rem(row, 4)

    def request(o):
        wanted = jnp.where(row < 4, list_ref[0, o], list_ref[1, o])
        valid = jnp.logical_and(wanted >= 0, comp < 3)
        req_ref[o] = jnp.where(valid, comp * stations + wanted, -1)

    list_copy.wait()
    each(0, n, request)
    pl.semaphore_wait(barrier, n - 1)

    def ask(d):
        peer = lax.rem(me + d, n)
        return push(req_ref.at[peer], asked.at[me], s1.at[d], r1.at[d], peer)

    def give(d):
        peer = lax.rem(me + d, n)
        return push(stage.at[peer], rx_ref.at[me], s2.at[d], r2.at[d], peer)

    def tell(d):
        peer = lax.rem(me + d, n)
        return push(mine, held.at[me], s3.at[d], r3.at[d], peer)

    each(1, n, lambda d: ask(d).start())
    ids[0:8, :] = jnp.full((8, LANES), -1, jnp.int32)
    ids[8:16, :] = jnp.zeros((8, LANES), jnp.int32)
    slots_copy.wait()
    moves_copy.wait()
    for k in range(sets):
        ids[0:1, k * nstat : (k + 1) * nstat] = slots_ref[k : k + 1, :]
        ids[8:9, k * nstat : (k + 1) * nstat] = moves_ref[k : k + 1, :]
    asked[me] = req_ref[me]

    tm_copy.wait()
    for c in range(3):
        for k in range(sets):
            hs[c, k * nstat : (k + 1) * nstat, :taps] = tm_ref[k, c].astype(jnp.float32)
        for v in range(ht.shape[1] // LANES):
            ht[c, v * LANES : (v + 1) * LANES, :] = hs[c, :, v * LANES : (v + 1) * LANES].T
        h = ht[c, :taps, :]
        tscale = jnp.sqrt(jnp.sum(h * h, axis=0, keepdims=True) / taps + 1e-05)
        tinv[c] = jnp.broadcast_to(1.0 / (taps * tscale), (8, LANES))

    rec_copy.wait()
    each(1, n, lambda d: ask(d).wait())
    rows = n * 8
    depth, width = rec_ref.shape
    want = asked[...].reshape(rows, LANES)[:, :depth]
    spot = lax.broadcasted_iota(jnp.int32, (rows, depth), 1)
    onehot = jnp.where(want == spot, 1.0, 0.0).astype(jnp.bfloat16)
    picked = jnp.dot(onehot, rec_ref[...], preferred_element_type=jnp.float32)
    stage[...] = picked.reshape(n, 8, width).astype(jnp.bfloat16)
    each(1, n, lambda d: give(d).start())
    rx_ref[me] = stage[me]

    each(1, n, lambda d: give(d).wait())

    spot = lax.broadcasted_iota(jnp.int32, (rows, LANES), 0)
    slot = ids[0:1, :] * 4
    chosen = jnp.concatenate(
        [jnp.where(spot == slot + c, 1.0, 0.0) for c in range(3)], axis=1
    ).astype(jnp.bfloat16)
    got = rx_ref[...].reshape(rows, width)
    picked = lax.dot_general(
        got, chosen, (((0,), (0,)), ((), ())), preferred_element_type=jnp.float32
    )
    for c in range(3):
        xs[c, :width, :] = picked[:, c * LANES : (c + 1) * LANES]

    moves = jnp.broadcast_to(ids[8:9, :], (8, LANES))
    bits = {b: (moves & b) != 0 for b in (128, 64, 32, 16, 8, 4, 2, 1)}

    def choose(bit, one, zero):
        return [jnp.where(bits[bit], p, q) for p, q in zip(one, zero)]

    def coarse(c, b):
        at = b * 64
        tiles = [xs[c, pl.ds(at + 8 * q, 8), :] for q in range(39)]
        for bit in (128, 64, 32, 16, 8):
            tiles = choose(bit, tiles[bit // 8 :], tiles[: -(bit // 8)])
        for q, tile in enumerate(tiles):
            ys[pl.ds(at + 8 * q, 8), :] = tile

    def fine(c, b):
        for q in range(5):
            at = b * 40 + 8 * q
            tiles = [ys[pl.ds(at + i, 8), :] for i in range(8)]
            for bit in (4, 2, 1):
                tiles = choose(bit, tiles[bit : 2 * bit], tiles[:bit])
            xt[c, pl.ds(at, 8), :] = tiles[0]

    def squares(c, at, count):
        total = None
        for i in range(count):
            x = xt[c, pl.ds(at + i, 8), :]
            total = x * x if total is None else total + x * x
        return total

    def eights(c, b):
        for q in range(4):
            at = b * 32 + 8 * q
            es[pl.ds(at, 8), :] = squares(c, at, 8)

    steps = taps // 8
    rest = taps - steps * 8

    def scales(c):
        run = [es[8 * q : 8 * q + 8, :] for q in range(OUT // 8 + steps - 1)]
        pieces = []
        size = 1
        while size <= steps:
            if steps & size:
                pieces.append((size, run))
            run = [p + q for p, q in zip(run, run[size:])]
            size *= 2
        for q in range(OUT // 8):
            done = 0
            total = squares(c, 8 * (q + steps), rest) if rest else None
            for size, piece in reversed(pieces):
                term = piece[q + done]
                total = term if total is None else total + term
                done += size
            it[c, 8 * q : 8 * q + 8, :] = lax.rsqrt(total / taps + 1e-05) * tinv[c]

    chan[...] = jnp.zeros_like(chan)
    tiles = 16
    span = tiles * 8

    def component(c):
        each(0, 9, lambda b: coarse(c, b))
        each(0, 14, lambda b: fine(c, b))
        each(0, 17, lambda b: eights(c, b))
        scales(c)
        for t0 in range(0, OUT, span):

            def phase(f, acc):
                win = [xt[c, pl.ds(t0 + f + 8 * q, 8), :] for q in range(tiles)]
                for e in range(steps):
                    h = jnp.broadcast_to(ht[c, pl.ds(f + 8 * e, 1), :], (8, LANES))
                    acc = tuple(a + h * w for a, w in zip(acc, win))
                    if e < steps - 1:
                        win = win[1:] + [xt[c, pl.ds(t0 + f + 8 * (tiles + e), 8), :]]
                return acc

            acc = tuple(jnp.zeros((8, LANES), jnp.float32) for _ in range(tiles))
            acc = lax.fori_loop(0, 8, phase, acc)
            for tap in range(taps // 8 * 8, taps):
                h = jnp.broadcast_to(ht[c, pl.ds(tap, 1), :], (8, LANES))
                acc = tuple(
                    a + h * xt[c, pl.ds(t0 + tap + 8 * q, 8), :] for q, a in enumerate(acc)
                )
            for q in range(tiles):
                at = pl.ds(t0 + 8 * q, 8)
                chan[at, :] += acc[q] * it[c, at, :]

    each(0, 3, component)
    flat = jnp.concatenate([chan[v : v + LANES].T for v in range(0, OUT, LANES)], axis=1)
    stack = jnp.concatenate(
        [jnp.sum(flat[k * nstat : (k + 1) * nstat], axis=0, keepdims=True) for k in range(sets)],
        axis=0,
    )
    stack_ref[...] = stack
    best = jnp.max(stack, axis=0, keepdims=True)
    mine[...] = best
    each(1, n, lambda d: tell(d).start())
    held[me] = best
    each(1, n, lambda d: tell(d).wait())
    peak_ref[...] = jnp.max(held[...], axis=0)


def on_device(records, templates, fetch_list, cluster_slots, moveouts):
    n = fetch_list.shape[1]
    stations, comps, width = records.shape
    sets, nstat = cluster_slots.shape
    taps = templates.shape[-1]
    padded = -(-taps // LANES) * LANES
    used = -(-(OUT + taps - 1) // LANES)
    rec_flat = jnp.transpose(records, (1, 0, 2)).reshape(comps * stations, width)
    kernels = jnp.transpose(templates, (0, 2, 1, 3))
    vmem = pl.BlockSpec(memory_space=pltpu.VMEM)
    far = pl.BlockSpec(memory_space=pltpu.HBM)
    sems = pltpu.SemaphoreType.DMA((n,))
    stack, peak = pl.pallas_call(
        functools.partial(kernel, n, stations, sets, nstat, taps),
        out_shape=(
            jax.ShapeDtypeStruct((sets, OUT), jnp.float32),
            jax.ShapeDtypeStruct((1, OUT), jnp.float32),
        ),
        in_specs=[far] * 5,
        out_specs=(vmem, vmem),
        scratch_shapes=[
            pltpu.SMEM((fetch_list.shape[2], n), jnp.int32),
            pltpu.VMEM(cluster_slots.shape, jnp.int32),
            pltpu.VMEM(moveouts.shape, jnp.int32),
            pltpu.VMEM(rec_flat.shape, jnp.bfloat16),
            pltpu.VMEM(kernels.shape, jnp.bfloat16),
            pltpu.VMEM((n, 8, LANES), jnp.int32),
            pltpu.VMEM((n, 8, LANES), jnp.int32),
            pltpu.VMEM((n, 8, width), jnp.bfloat16),
            pltpu.VMEM((n, 8, width), jnp.bfloat16),
            pltpu.VMEM((16, LANES), jnp.int32),
            pltpu.VMEM((3, 832, LANES), jnp.float32),
            pltpu.VMEM((576, LANES), jnp.float32),
            pltpu.VMEM((544, LANES), jnp.float32),
            pltpu.VMEM((3, used * LANES, LANES), jnp.float32),
            pltpu.VMEM((3, OUT, LANES), jnp.float32),
            pltpu.VMEM((3, LANES, padded), jnp.float32),
            pltpu.VMEM((3, padded, LANES), jnp.float32),
            pltpu.VMEM((3, 8, LANES), jnp.float32),
            pltpu.VMEM((OUT, LANES), jnp.float32),
            pltpu.VMEM((1, OUT), jnp.float32),
            pltpu.VMEM((n, 1, OUT), jnp.float32),
            pltpu.SemaphoreType.DMA((5,)),
            sems, sems, sems, sems, sems, sems,
        ],
        compiler_params=pltpu.CompilerParams(
            collective_id=0, has_side_effects=True, vmem_limit_bytes=60 << 20
        ),
        name="network_stack",
    )(jnp.transpose(fetch_list[0]), cluster_slots, moveouts, rec_flat, kernels)
    return stack, peak.reshape(OUT)


def solution(mesh):
    placed = (
        P(("groups", "tmpl"), None, None),
        P("tmpl", None, None, None),
        P("tmpl", None, None),
        P("tmpl", None),
        P("tmpl", None),
    )
    return jax.shard_map(
        on_device,
        mesh=mesh,
        in_specs=placed,
        out_specs=(P(("groups", "tmpl"), None), P("groups")),
        check_vma=False,
    )
```

```python
import functools

import jax
import jax.numpy as jnp
from jax import lax
from jax.experimental import pallas as pl
from jax.experimental.pallas import tpu as pltpu
from jax.sharding import PartitionSpec as P

OUT = 256
LANES = 128


def push(src, dst, send, recv, peer):
    return pltpu.make_async_remote_copy(
        src_ref=src,
        dst_ref=dst,
        send_sem=send,
        recv_sem=recv,
        device_id={"tmpl": peer},
        device_id_type=pl.DeviceIdType.MESH,
    )


def each(low, high, action):
    def body(d, carry):
        action(d)
        return carry

    lax.fori_loop(low, high, body, 0)


def kernel(
    n, stations, sets, nstat, taps,
    list_hbm, slots_hbm, moves_hbm, rec_hbm, tm_hbm,
    stack_ref, peak_ref,
    list_ref, slots_ref, moves_ref, rec_ref, tm_ref, req_ref, asked, stage, rx_ref, ids, xs, ys, es, xt, it, hs, ht, tinv, xa, ha, af, line, chan, mine, held,
    local, s1, r1, s2, r2, s3, r3,
):
    me = lax.axis_index("tmpl")
    tm_copy = pltpu.make_async_copy(tm_hbm, tm_ref, local.at[0])
    rec_copy = pltpu.make_async_copy(rec_hbm, rec_ref, local.at[1])
    list_copy = pltpu.make_async_copy(list_hbm, list_ref, local.at[2])
    slots_copy = pltpu.make_async_copy(slots_hbm, slots_ref, local.at[3])
    moves_copy = pltpu.make_async_copy(moves_hbm, moves_ref, local.at[4])
    list_copy.start()
    rec_copy.start()
    slots_copy.start()
    moves_copy.start()
    tm_copy.start()

    rx_ref[...] = jnp.zeros_like(rx_ref)
    barrier = pltpu.get_barrier_semaphore()
    each(1, n, lambda d: pl.semaphore_signal(
        barrier, inc=1, device_id={"tmpl": lax.rem(me + d, n)},
        device_id_type=pl.DeviceIdType.MESH))

    row = lax.broadcasted_iota(jnp.int32, (8, LANES), 0)
    comp = jnp.where(row < 3, row, row - 3)

    def request(o):
        wanted = jnp.where(row < 3, list_ref[0, o], list_ref[1, o])
        valid = jnp.logical_and(wanted >= 0, row < 6)
        req_ref[o] = jnp.where(valid, comp * stations + wanted, -1)

    list_copy.wait()
    each(0, n, request)
    pl.semaphore_wait(barrier, n - 1)

    def ask(d):
        peer = lax.rem(me + d, n)
        return push(req_ref.at[peer], asked.at[me], s1.at[d], r1.at[d], peer)

    def give(d):
        peer = lax.rem(me + d, n)
        return push(stage.at[peer, pl.ds(0, 6)], rx_ref.at[me, pl.ds(0, 6)], s2.at[d], r2.at[d], peer)

    def tell(d):
        peer = lax.rem(me + d, n)
        return push(mine, held.at[me], s3.at[d], r3.at[d], peer)

    each(1, n, lambda d: ask(d).start())
    ids[0:8, :] = jnp.full((8, LANES), -1, jnp.int32)
    ids[8:16, :] = jnp.zeros((8, LANES), jnp.int32)
    slots_copy.wait()
    moves_copy.wait()
    for k in range(sets):
        ids[0:1, k * nstat : (k + 1) * nstat] = slots_ref[k : k + 1, :]
        ids[8:9, k * nstat : (k + 1) * nstat] = moves_ref[k : k + 1, :]
    asked[me] = req_ref[me]

    tm_copy.wait()
    for c in range(3):
        for k in range(sets):
            hs[c, k * nstat : (k + 1) * nstat, :taps] = tm_ref[k, c].astype(jnp.float32)
        for v in range(ht.shape[1] // LANES):
            ht[c, v * LANES : (v + 1) * LANES, :] = hs[c, :, v * LANES : (v + 1) * LANES].T
        h0 = ht[c, pl.ds(0, taps // 2, stride=2), :]
        h1 = ht[c, pl.ds(1, taps // 2, stride=2), :]
        ha[c, 0, : taps // 2, :] = h0 + h1
        ha[c, 1, : taps // 2, :] = h0
        ha[c, 2, : taps // 2, :] = h1
        h = ht[c, :taps, :]
        tscale = jnp.sqrt(jnp.sum(h * h, axis=0, keepdims=True) / taps + 1e-05)
        tinv[c] = jnp.broadcast_to(1.0 / (taps * tscale), (8, LANES))

    rec_copy.wait()
    each(1, n, lambda d: ask(d).wait())
    rows = n * 8
    depth, width = rec_ref.shape
    want = asked[...].reshape(rows, LANES)[:, :depth]
    spot = lax.broadcasted_iota(jnp.int32, (rows, depth), 1)
    onehot = jnp.where(want == spot, 1.0, 0.0).astype(jnp.bfloat16)
    picked = jnp.dot(onehot, rec_ref[...], preferred_element_type=jnp.float32)
    stage[...] = picked.reshape(n, 8, width).astype(jnp.bfloat16)
    each(1, n, lambda d: give(d).start())
    rx_ref[me] = stage[me]

    each(1, n, lambda d: give(d).wait())

    spot = lax.broadcasted_iota(jnp.int32, (rows, LANES), 0)
    slot = (ids[0:1, :] >> 1) * 8 + (ids[0:1, :] & 1) * 3
    chosen = jnp.concatenate(
        [jnp.where(spot == slot + c, 1.0, 0.0) for c in range(3)], axis=1
    ).astype(jnp.bfloat16)
    got = rx_ref[...].reshape(rows, width)
    picked = lax.dot_general(
        got, chosen, (((0,), (0,)), ((), ())), preferred_element_type=jnp.float32
    )
    for c in range(3):
        xs[c, :width, :] = picked[:, c * LANES : (c + 1) * LANES]

    moves = jnp.broadcast_to(ids[8:9, :], (8, LANES))
    bits = {b: (moves & b) != 0 for b in (128, 64, 32, 16, 8, 4, 2, 1)}

    def choose(bit, one, zero):
        return [jnp.where(bits[bit], p, q) for p, q in zip(one, zero)]

    def coarse(c, b):
        at = b * 64
        tiles = [xs[c, pl.ds(at + 8 * q, 8), :] for q in range(39)]
        for bit in (128, 64, 32, 16, 8):
            tiles = choose(bit, tiles[bit // 8 :], tiles[: -(bit // 8)])
        for q, tile in enumerate(tiles):
            ys[pl.ds(at + 8 * q, 8), :] = tile

    def fine(c, b):
        for q in range(5):
            at = b * 40 + 8 * q
            tiles = [ys[pl.ds(at + i, 8), :] for i in range(8)]
            for bit in (4, 2, 1):
                tiles = choose(bit, tiles[bit : 2 * bit], tiles[:bit])
            xt[c, pl.ds(at, 8), :] = tiles[0]

    def squares(c, at, count):
        total = None
        for i in range(count):
            x = xt[c, pl.ds(at + i, 8), :]
            total = x * x if total is None else total + x * x
        return total

    def eights(c, b):
        for q in range(4):
            at = b * 32 + 8 * q
            es[pl.ds(at, 8), :] = squares(c, at, 8)

    steps = taps // 8
    rest = taps - steps * 8

    def scales(c):
        run = [es[8 * q : 8 * q + 8, :] for q in range(OUT // 8 + steps - 1)]
        pieces = []
        size = 1
        while size <= steps:
            if steps & size:
                pieces.append((size, run))
            run = [p + q for p, q in zip(run, run[size:])]
            size *= 2
        for q in range(OUT // 8):
            done = 0
            total = squares(c, 8 * (q + steps), rest) if rest else None
            for size, piece in reversed(pieces):
                term = piece[q + done]
                total = term if total is None else total + term
                done += size
            it[c, 8 * q : 8 * q + 8, :] = lax.rsqrt(total / taps + 1e-05) * tinv[c]

    chan[...] = jnp.zeros_like(chan)
    tiles = 16

    def parts(c, b):
        for q in range(5):
            at = b * 40 + 8 * q
            x0 = xt[c, pl.ds(2 * at, 8, stride=2), :]
            x1 = xt[c, pl.ds(2 * at + 1, 8, stride=2), :]
            x2 = xt[c, pl.ds(2 * at + 2, 8, stride=2), :]
            xa[0, pl.ds(at, 8), :] = x1
            xa[1, pl.ds(at, 8), :] = x0 - x1
            xa[2, pl.ds(at, 8), :] = x2 - x1

    def correlate(c, m):
        def phase(count):
            def body(f, acc):
                win = [xa[m, pl.ds(f + 8 * q, 8), :] for q in range(tiles)]
                for e in range(count):
                    h = jnp.broadcast_to(ha[c, m, pl.ds(f + 8 * e, 1), :], (8, LANES))
                    acc = tuple(a + h * w for a, w in zip(acc, win))
                    if e < count - 1:
                        win = win[1:] + [xa[m, pl.ds(f + 8 * (tiles + e), 8), :]]
                return acc

            return body

        taken = taps // 2
        acc = tuple(jnp.zeros((8, LANES), jnp.float32) for _ in range(tiles))
        acc = lax.fori_loop(0, taken % 8, phase(taken // 8 + 1), acc)
        acc = lax.fori_loop(taken % 8, 8, phase(taken // 8), acc)
        for q in range(tiles):
            af[m, 8 * q : 8 * q + 8, :] = acc[q]

    def component(c):
        each(0, 9, lambda b: coarse(c, b))
        each(0, 14, lambda b: fine(c, b))
        each(0, 17, lambda b: eights(c, b))
        scales(c)
        each(0, 7, lambda b: parts(c, b))
        each(0, 3, lambda m: correlate(c, m))
        for q in range(tiles):
            at = slice(8 * q, 8 * q + 8)
            common = af[0, at, :]
            even = it[c, pl.ds(16 * q, 8, stride=2), :]
            odd = it[c, pl.ds(16 * q + 1, 8, stride=2), :]
            chan[0, at, :] += (common + af[1, at, :]) * even
            chan[1, at, :] += (common + af[2, at, :]) * odd

    each(0, 3, component)
    for q in range(tiles):
        line[pl.ds(16 * q, 8, stride=2), :] = chan[0, 8 * q : 8 * q + 8, :]
        line[pl.ds(16 * q + 1, 8, stride=2), :] = chan[1, 8 * q : 8 * q + 8, :]
    flat = jnp.concatenate([line[v : v + LANES, :].T for v in range(0, OUT, LANES)], axis=1)
    stack = jnp.concatenate(
        [jnp.sum(flat[k * nstat : (k + 1) * nstat], axis=0, keepdims=True) for k in range(sets)],
        axis=0,
    )
    stack_ref[...] = stack
    best = jnp.max(stack, axis=0, keepdims=True)
    mine[...] = best
    each(1, n, lambda d: tell(d).start())
    held[me] = best
    each(1, n, lambda d: tell(d).wait())
    peak_ref[...] = jnp.max(held[...], axis=0)


def on_device(records, templates, fetch_list, cluster_slots, moveouts):
    n = fetch_list.shape[1]
    stations, comps, width = records.shape
    sets, nstat = cluster_slots.shape
    taps = templates.shape[-1]
    padded = -(-taps // LANES) * LANES
    used = -(-(OUT + taps - 1) // LANES)
    rec_flat = jnp.transpose(records, (1, 0, 2)).reshape(comps * stations, width)
    kernels = jnp.transpose(templates, (0, 2, 1, 3))
    vmem = pl.BlockSpec(memory_space=pltpu.VMEM)
    far = pl.BlockSpec(memory_space=pltpu.HBM)
    sems = pltpu.SemaphoreType.DMA((n,))
    stack, peak = pl.pallas_call(
        functools.partial(kernel, n, stations, sets, nstat, taps),
        out_shape=(
            jax.ShapeDtypeStruct((sets, OUT), jnp.float32),
            jax.ShapeDtypeStruct((1, OUT), jnp.float32),
        ),
        in_specs=[far] * 5,
        out_specs=(vmem, vmem),
        scratch_shapes=[
            pltpu.SMEM((fetch_list.shape[2], n), jnp.int32),
            pltpu.VMEM(cluster_slots.shape, jnp.int32),
            pltpu.VMEM(moveouts.shape, jnp.int32),
            pltpu.VMEM(rec_flat.shape, jnp.bfloat16),
            pltpu.VMEM(kernels.shape, jnp.bfloat16),
            pltpu.VMEM((n, 8, LANES), jnp.int32),
            pltpu.VMEM((n, 8, LANES), jnp.int32),
            pltpu.VMEM((n, 8, width), jnp.bfloat16),
            pltpu.VMEM((n, 8, width), jnp.bfloat16),
            pltpu.VMEM((16, LANES), jnp.int32),
            pltpu.VMEM((3, 832, LANES), jnp.float32),
            pltpu.VMEM((576, LANES), jnp.float32),
            pltpu.VMEM((544, LANES), jnp.float32),
            pltpu.VMEM((3, used * LANES, LANES), jnp.float32),
            pltpu.VMEM((3, OUT, LANES), jnp.float32),
            pltpu.VMEM((3, LANES, padded), jnp.float32),
            pltpu.VMEM((3, padded, LANES), jnp.float32),
            pltpu.VMEM((3, 8, LANES), jnp.float32),
            pltpu.VMEM((3, 280, LANES), jnp.float32),
            pltpu.VMEM((3, 3, padded // 2, LANES), jnp.float32),
            pltpu.VMEM((3, OUT // 2, LANES), jnp.float32),
            pltpu.VMEM((OUT, LANES), jnp.float32),
            pltpu.VMEM((2, OUT // 2, LANES), jnp.float32),
            pltpu.VMEM((1, OUT), jnp.float32),
            pltpu.VMEM((n, 1, OUT), jnp.float32),
            pltpu.SemaphoreType.DMA((5,)),
            sems, sems, sems, sems, sems, sems,
        ],
        compiler_params=pltpu.CompilerParams(
            collective_id=0, has_side_effects=True, vmem_limit_bytes=60 << 20
        ),
        name="network_stack",
    )(jnp.transpose(fetch_list[0]), cluster_slots, moveouts, rec_flat, kernels)
    return stack, peak.reshape(OUT)


def solution(mesh):
    placed = (
        P(("groups", "tmpl"), None, None),
        P("tmpl", None, None, None),
        P("tmpl", None, None),
        P("tmpl", None),
        P("tmpl", None),
    )
    return jax.shard_map(
        on_device,
        mesh=mesh,
        in_specs=placed,
        out_specs=(P(("groups", "tmpl"), None), P("groups")),
        check_vma=False,
    )
```

```python
import functools

import jax
import jax.numpy as jnp
from jax import lax
from jax.experimental import pallas as pl
from jax.experimental.pallas import tpu as pltpu
from jax.sharding import PartitionSpec as P

OUT = 256
LANES = 128


def push(src, dst, send, recv, peer):
    return pltpu.make_async_remote_copy(
        src_ref=src,
        dst_ref=dst,
        send_sem=send,
        recv_sem=recv,
        device_id={"tmpl": peer},
        device_id_type=pl.DeviceIdType.MESH,
    )


def each(low, high, action):
    def body(d, carry):
        action(d)
        return carry

    lax.fori_loop(low, high, body, 0)


def kernel(
    n, stations, sets, nstat, taps,
    list_hbm, slots_hbm, moves_hbm, rec_hbm, tm_hbm,
    stack_ref, peak_ref,
    list_ref, slots_ref, moves_ref, rec_ref, tm_ref, req_ref, asked, stage, rx_ref, ids, xs, ys, es, xt, it, hs, ht, tinv, xa, ha, af, line, chan, mine, held,
    local, s1, r1, s2, r2, s3, r3,
):
    me = lax.axis_index("tmpl")
    tm_copy = pltpu.make_async_copy(tm_hbm, tm_ref, local.at[0])
    rec_copy = pltpu.make_async_copy(rec_hbm, rec_ref, local.at[1])
    list_copy = pltpu.make_async_copy(list_hbm, list_ref, local.at[2])
    slots_copy = pltpu.make_async_copy(slots_hbm, slots_ref, local.at[3])
    moves_copy = pltpu.make_async_copy(moves_hbm, moves_ref, local.at[4])
    list_copy.start()
    rec_copy.start()
    slots_copy.start()
    moves_copy.start()
    tm_copy.start()

    barrier = pltpu.get_barrier_semaphore()
    each(1, n, lambda d: pl.semaphore_signal(
        barrier, inc=1, device_id={"tmpl": lax.rem(me + d, n)},
        device_id_type=pl.DeviceIdType.MESH))

    lane = lax.broadcasted_iota(jnp.int32, (1, LANES), 1)

    def request(o):
        req_ref[o] = jnp.where(lane % 2 == 0, list_ref[0, o], list_ref[1, o])

    list_copy.wait()
    each(0, n, request)
    pl.semaphore_wait(barrier, n - 1)

    def ask(d):
        peer = lax.rem(me + d, n)
        return push(req_ref.at[peer], asked.at[me], s1.at[d], r1.at[d], peer)

    def give(c, d):
        peer = lax.rem(me + d, n)
        return push(stage.at[c, peer], rx_ref.at[c, me], s2.at[c, d], r2.at[c, d], peer)

    def tell(d):
        peer = lax.rem(me + d, n)
        return push(mine, held.at[me], s3.at[d], r3.at[d], peer)

    each(1, n, lambda d: ask(d).start())
    ids[0:8, :] = jnp.full((8, LANES), -1, jnp.int32)
    ids[8:16, :] = jnp.zeros((8, LANES), jnp.int32)
    slots_copy.wait()
    moves_copy.wait()
    for k in range(sets):
        ids[0:1, k * nstat : (k + 1) * nstat] = slots_ref[k : k + 1, :]
        ids[8:9, k * nstat : (k + 1) * nstat] = moves_ref[k : k + 1, :]
    asked[me] = req_ref[me]

    tm_copy.wait()
    for c in range(3):
        for k in range(sets):
            hs[c, k * nstat : (k + 1) * nstat, :taps] = tm_ref[k, c].astype(jnp.float32)
        for v in range(ht.shape[1] // LANES):
            ht[c, v * LANES : (v + 1) * LANES, :] = hs[c, :, v * LANES : (v + 1) * LANES].T
        h0 = ht[c, pl.ds(0, taps // 2, stride=2), :]
        h1 = ht[c, pl.ds(1, taps // 2, stride=2), :]
        ha[c, 0, : taps // 2, :] = h0 + h1
        ha[c, 1, : taps // 2, :] = h0
        ha[c, 2, : taps // 2, :] = h1
        h = ht[c, :taps, :]
        tscale = jnp.sqrt(jnp.sum(h * h, axis=0, keepdims=True) / taps + 1e-05)
        tinv[c] = jnp.broadcast_to(1.0 / (taps * tscale), (8, LANES))

    rec_copy.wait()
    each(1, n, lambda d: ask(d).wait())
    width = rec_ref.shape[1]
    slots = 2 * n
    share = LANES // 2
    asks = asked[...].reshape(n, LANES)
    wants = []
    for first in range(0, n, share):
        some = asks[first : first + share]
        holder = lax.broadcasted_iota(jnp.int32, some.shape, 0)
        column = lax.broadcasted_iota(jnp.int32, some.shape, 1)
        mine_here = jnp.where(column // 2 == holder, some, 0)
        wants.append(jnp.sum(mine_here, axis=0, keepdims=True)[:, : 2 * some.shape[0]])
    want = jnp.concatenate(wants, axis=1) if len(wants) > 1 else wants[0]
    spot = lax.broadcasted_iota(jnp.int32, (stations, slots), 0)
    onehot = jnp.where(spot == want, 1.0, 0.0).astype(jnp.bfloat16)
    for c in range(3):
        picked = lax.dot_general(
            onehot,
            rec_ref[c * stations : (c + 1) * stations, :],
            (((0,), (0,)), ((), ())),
            preferred_element_type=jnp.float32,
        )
        stage[c] = picked.reshape(n, 2, width).astype(jnp.bfloat16)
        each(1, n, functools.partial(lambda c, d: give(c, d).start(), c))
        rx_ref[c, me] = stage[c, me]

    spot = lax.broadcasted_iota(jnp.int32, (slots, LANES), 0)
    chosen = jnp.where(spot == ids[0:1, :], 1.0, 0.0).astype(jnp.bfloat16)

    def gather(c):
        each(1, n, lambda d: give(c, d).wait())
        got = rx_ref[c].astype(jnp.float32).reshape(slots, width).astype(jnp.bfloat16)
        xs[c, :width, :] = lax.dot_general(
            got, chosen, (((0,), (0,)), ((), ())), preferred_element_type=jnp.float32
        )

    moves = jnp.broadcast_to(ids[8:9, :], (8, LANES))
    bits = {b: (moves & b) != 0 for b in (128, 64, 32, 16, 8, 4, 2, 1)}

    def choose(bit, one, zero):
        return [jnp.where(bits[bit], p, q) for p, q in zip(one, zero)]

    def coarse(c, b):
        at = b * 64
        tiles = [xs[c, pl.ds(at + 8 * q, 8), :] for q in range(39)]
        for bit in (128, 64, 32, 16, 8):
            tiles = choose(bit, tiles[bit // 8 :], tiles[: -(bit // 8)])
        for q, tile in enumerate(tiles):
            ys[pl.ds(at + 8 * q, 8), :] = tile

    def fine(c, b):
        for q in range(5):
            at = b * 40 + 8 * q
            tiles = [ys[pl.ds(at + i, 8), :] for i in range(8)]
            for bit in (4, 2, 1):
                tiles = choose(bit, tiles[bit : 2 * bit], tiles[:bit])
            xt[c, pl.ds(at, 8), :] = tiles[0]

    def squares(c, at, count):
        total = None
        for i in range(count):
            x = xt[c, pl.ds(at + i, 8), :]
            total = x * x if total is None else total + x * x
        return total

    def eights(c, b):
        for q in range(4):
            at = b * 32 + 8 * q
            es[pl.ds(at, 8), :] = squares(c, at, 8)

    steps = taps // 8
    rest = taps - steps * 8

    def scales(c):
        run = [es[8 * q : 8 * q + 8, :] for q in range(OUT // 8 + steps - 1)]
        pieces = []
        size = 1
        while size <= steps:
            if steps & size:
                pieces.append((size, run))
            run = [p + q for p, q in zip(run, run[size:])]
            size *= 2
        for q in range(OUT // 8):
            done = 0
            total = squares(c, 8 * (q + steps), rest) if rest else None
            for size, piece in reversed(pieces):
                term = piece[q + done]
                total = term if total is None else total + term
                done += size
            it[c, 8 * q : 8 * q + 8, :] = lax.rsqrt(total / taps + 1e-05) * tinv[c]

    chan[...] = jnp.zeros_like(chan)
    tiles = 16

    def parts(c, b):
        for q in range(5):
            at = b * 40 + 8 * q
            x0 = xt[c, pl.ds(2 * at, 8, stride=2), :]
            x1 = xt[c, pl.ds(2 * at + 1, 8, stride=2), :]
            x2 = xt[c, pl.ds(2 * at + 2, 8, stride=2), :]
            xa[0, pl.ds(at, 8), :] = x1
            xa[1, pl.ds(at, 8), :] = x0 - x1
            xa[2, pl.ds(at, 8), :] = x2 - x1

    def correlate(c, m):
        def phase(count):
            def body(f, acc):
                win = [xa[m, pl.ds(f + 8 * q, 8), :] for q in range(tiles)]
                for e in range(count):
                    h = jnp.broadcast_to(ha[c, m, pl.ds(f + 8 * e, 1), :], (8, LANES))
                    acc = tuple(a + h * w for a, w in zip(acc, win))
                    if e < count - 1:
                        win = win[1:] + [xa[m, pl.ds(f + 8 * (tiles + e), 8), :]]
                return acc

            return body

        taken = taps // 2
        acc = tuple(jnp.zeros((8, LANES), jnp.float32) for _ in range(tiles))
        acc = lax.fori_loop(0, taken % 8, phase(taken // 8 + 1), acc)
        acc = lax.fori_loop(taken % 8, 8, phase(taken // 8), acc)
        for q in range(tiles):
            af[m, 8 * q : 8 * q + 8, :] = acc[q]

    def component(c):
        gather(c)
        each(0, 9, lambda b: coarse(c, b))
        each(0, 14, lambda b: fine(c, b))
        each(0, 17, lambda b: eights(c, b))
        scales(c)
        each(0, 7, lambda b: parts(c, b))
        each(0, 3, lambda m: correlate(c, m))
        for q in range(tiles):
            at = slice(8 * q, 8 * q + 8)
            common = af[0, at, :]
            even = it[c, pl.ds(16 * q, 8, stride=2), :]
            odd = it[c, pl.ds(16 * q + 1, 8, stride=2), :]
            chan[0, at, :] += (common + af[1, at, :]) * even
            chan[1, at, :] += (common + af[2, at, :]) * odd

    each(0, 3, component)
    for q in range(tiles):
        line[pl.ds(16 * q, 8, stride=2), :] = chan[0, 8 * q : 8 * q + 8, :]
        line[pl.ds(16 * q + 1, 8, stride=2), :] = chan[1, 8 * q : 8 * q + 8, :]
    flat = jnp.concatenate([line[v : v + LANES, :].T for v in range(0, OUT, LANES)], axis=1)
    stack = jnp.concatenate(
        [jnp.sum(flat[k * nstat : (k + 1) * nstat], axis=0, keepdims=True) for k in range(sets)],
        axis=0,
    )
    stack_ref[...] = stack
    best = jnp.max(stack, axis=0, keepdims=True)
    mine[...] = best
    each(1, n, lambda d: tell(d).start())
    held[me] = best
    each(1, n, lambda d: tell(d).wait())
    peak_ref[...] = jnp.max(held[...], axis=0)


def on_device(records, templates, fetch_list, cluster_slots, moveouts):
    n = fetch_list.shape[1]
    stations, comps, width = records.shape
    sets, nstat = cluster_slots.shape
    taps = templates.shape[-1]
    padded = -(-taps // LANES) * LANES
    used = -(-(OUT + taps - 1) // LANES)
    rec_flat = jnp.transpose(records, (1, 0, 2)).reshape(comps * stations, width)
    kernels = jnp.transpose(templates, (0, 2, 1, 3))
    vmem = pl.BlockSpec(memory_space=pltpu.VMEM)
    far = pl.BlockSpec(memory_space=pltpu.HBM)
    many = pltpu.SemaphoreType.DMA((3, n))
    sems = pltpu.SemaphoreType.DMA((n,))
    stack, peak = pl.pallas_call(
        functools.partial(kernel, n, stations, sets, nstat, taps),
        out_shape=(
            jax.ShapeDtypeStruct((sets, OUT), jnp.float32),
            jax.ShapeDtypeStruct((1, OUT), jnp.float32),
        ),
        in_specs=[far] * 5,
        out_specs=(vmem, vmem),
        scratch_shapes=[
            pltpu.SMEM((fetch_list.shape[2], n), jnp.int32),
            pltpu.VMEM(cluster_slots.shape, jnp.int32),
            pltpu.VMEM(moveouts.shape, jnp.int32),
            pltpu.VMEM(rec_flat.shape, jnp.bfloat16),
            pltpu.VMEM(kernels.shape, jnp.bfloat16),
            pltpu.VMEM((n, 1, LANES), jnp.int32),
            pltpu.VMEM((n, 1, LANES), jnp.int32),
            pltpu.VMEM((3, n, 2, width), jnp.bfloat16),
            pltpu.VMEM((3, n, 2, width), jnp.bfloat16),
            pltpu.VMEM((16, LANES), jnp.int32),
            pltpu.VMEM((3, 832, LANES), jnp.float32),
            pltpu.VMEM((576, LANES), jnp.float32),
            pltpu.VMEM((544, LANES), jnp.float32),
            pltpu.VMEM((3, used * LANES, LANES), jnp.float32),
            pltpu.VMEM((3, OUT, LANES), jnp.float32),
            pltpu.VMEM((3, LANES, padded), jnp.float32),
            pltpu.VMEM((3, padded, LANES), jnp.float32),
            pltpu.VMEM((3, 8, LANES), jnp.float32),
            pltpu.VMEM((3, 280, LANES), jnp.float32),
            pltpu.VMEM((3, 3, padded // 2, LANES), jnp.float32),
            pltpu.VMEM((3, OUT // 2, LANES), jnp.float32),
            pltpu.VMEM((OUT, LANES), jnp.float32),
            pltpu.VMEM((2, OUT // 2, LANES), jnp.float32),
            pltpu.VMEM((1, OUT), jnp.float32),
            pltpu.VMEM((n, 1, OUT), jnp.float32),
            pltpu.SemaphoreType.DMA((5,)),
            sems, sems, many, many, sems, sems,
        ],
        compiler_params=pltpu.CompilerParams(
            collective_id=0, has_side_effects=True, vmem_limit_bytes=60 << 20
        ),
        name="network_stack",
    )(jnp.transpose(fetch_list[0]), cluster_slots, moveouts, rec_flat, kernels)
    return stack, peak.reshape(OUT)


def solution(mesh):
    placed = (
        P(("groups", "tmpl"), None, None),
        P("tmpl", None, None, None),
        P("tmpl", None, None),
        P("tmpl", None),
        P("tmpl", None),
    )
    return jax.shard_map(
        on_device,
        mesh=mesh,
        in_specs=placed,
        out_specs=(P(("groups", "tmpl"), None), P("groups")),
        check_vma=False,
    )
```

```python
import functools

import jax
import jax.numpy as jnp
from jax import lax
from jax.experimental import pallas as pl
from jax.experimental.pallas import tpu as pltpu
from jax.sharding import PartitionSpec as P

OUT = 256
LANES = 128


def push(src, dst, send, recv, peer):
    return pltpu.make_async_remote_copy(
        src_ref=src,
        dst_ref=dst,
        send_sem=send,
        recv_sem=recv,
        device_id={"tmpl": peer},
        device_id_type=pl.DeviceIdType.MESH,
    )


def each(low, high, action):
    def body(d, carry):
        action(d)
        return carry

    lax.fori_loop(low, high, body, 0)


def kernel(
    n, stations, sets, nstat, taps,
    list_hbm, slots_hbm, moves_hbm, rec_hbm, tm_hbm,
    stack_ref, peak_ref,
    list_ref, slots_ref, moves_ref, rec_ref, tm_ref, req_ref, asked, stage, rx_ref, ids, xs, ys, es, xt, it, hs, ht, tinv, xa, ha, af, line, chan, mine, held,
    local, s1, r1, s2, r2, s3, r3,
):
    me = lax.axis_index("tmpl")
    tm_copy = pltpu.make_async_copy(tm_hbm, tm_ref, local.at[0])
    rec_copy = pltpu.make_async_copy(rec_hbm, rec_ref, local.at[1])
    list_copy = pltpu.make_async_copy(list_hbm, list_ref, local.at[2])
    slots_copy = pltpu.make_async_copy(slots_hbm, slots_ref, local.at[3])
    moves_copy = pltpu.make_async_copy(moves_hbm, moves_ref, local.at[4])
    list_copy.start()
    rec_copy.start()
    slots_copy.start()
    moves_copy.start()
    tm_copy.start()

    barrier = pltpu.get_barrier_semaphore()
    each(1, n, lambda d: pl.semaphore_signal(
        barrier, inc=1, device_id={"tmpl": lax.rem(me + d, n)},
        device_id_type=pl.DeviceIdType.MESH))

    lane = lax.broadcasted_iota(jnp.int32, (1, LANES), 1)

    def request(o):
        req_ref[o] = jnp.where(lane % 2 == 0, list_ref[0, o], list_ref[1, o])

    list_copy.wait()
    each(0, n, request)
    pl.semaphore_wait(barrier, n - 1)

    def ask(d):
        peer = lax.rem(me + d, n)
        return push(req_ref.at[peer], asked.at[me], s1.at[d], r1.at[d], peer)

    def give(m, d):
        part = pl.ds(0, 1) if m == 0 else pl.ds(1, 2)
        peer = lax.rem(me + d, n)
        return push(stage.at[part, peer], rx_ref.at[part, me], s2.at[m, d], r2.at[m, d], peer)

    def tell(d):
        peer = lax.rem(me + d, n)
        return push(mine, held.at[me], s3.at[d], r3.at[d], peer)

    each(1, n, lambda d: ask(d).start())
    ids[0:8, :] = jnp.full((8, LANES), -1, jnp.int32)
    ids[8:16, :] = jnp.zeros((8, LANES), jnp.int32)
    slots_copy.wait()
    moves_copy.wait()
    for k in range(sets):
        ids[0:1, k * nstat : (k + 1) * nstat] = slots_ref[k : k + 1, :]
        ids[8:9, k * nstat : (k + 1) * nstat] = moves_ref[k : k + 1, :]
    asked[me] = req_ref[me]

    tm_copy.wait()
    for c in range(3):
        for k in range(sets):
            hs[c, k * nstat : (k + 1) * nstat, :taps] = tm_ref[k, c].astype(jnp.float32)
        for v in range(ht.shape[1] // LANES):
            ht[c, v * LANES : (v + 1) * LANES, :] = hs[c, :, v * LANES : (v + 1) * LANES].T
        h0 = ht[c, pl.ds(0, taps // 2, stride=2), :]
        h1 = ht[c, pl.ds(1, taps // 2, stride=2), :]
        ha[c, 0, : taps // 2, :] = h0 + h1
        ha[c, 1, : taps // 2, :] = h0
        ha[c, 2, : taps // 2, :] = h1
        h = ht[c, :taps, :]
        tscale = jnp.sqrt(jnp.sum(h * h, axis=0, keepdims=True) / taps + 1e-05)
        tinv[c] = jnp.broadcast_to(1.0 / (taps * tscale), (8, LANES))

    rec_copy.wait()
    each(1, n, lambda d: ask(d).wait_recv())
    width = rec_ref.shape[1]
    slots = 2 * n
    share = LANES // 2
    asks = asked[...].reshape(n, LANES)
    wants = []
    for first in range(0, n, share):
        some = asks[first : first + share]
        holder = lax.broadcasted_iota(jnp.int32, some.shape, 0)
        column = lax.broadcasted_iota(jnp.int32, some.shape, 1)
        mine_here = jnp.where(column // 2 == holder, some, 0)
        wants.append(jnp.sum(mine_here, axis=0, keepdims=True)[:, : 2 * some.shape[0]])
    want = jnp.concatenate(wants, axis=1) if len(wants) > 1 else wants[0]
    spot = lax.broadcasted_iota(jnp.int32, (stations, slots), 0)
    onehot = jnp.where(spot == want, 1.0, 0.0).astype(jnp.bfloat16)
    for c in range(3):
        picked = lax.dot_general(
            onehot,
            rec_ref[c * stations : (c + 1) * stations, :],
            (((0,), (0,)), ((), ())),
            preferred_element_type=jnp.float32,
        )
        stage[c] = picked.reshape(n, 2, width).astype(jnp.bfloat16)
        if c == 0:
            each(1, n, lambda d: give(0, d).start())
        if c == 2:
            each(1, n, lambda d: give(1, d).start())
        rx_ref[c, me] = stage[c, me]

    spot = lax.broadcasted_iota(jnp.int32, (slots, LANES), 0)
    chosen = jnp.where(spot == ids[0:1, :], 1.0, 0.0).astype(jnp.bfloat16)

    def gather(c):
        @pl.when(c == 0)
        def _():
            each(1, n, lambda d: give(0, d).wait_recv())

        @pl.when(c == 1)
        def _():
            each(1, n, lambda d: give(1, d).wait_recv())

        got = rx_ref[c].astype(jnp.float32).reshape(slots, width).astype(jnp.bfloat16)
        xs[c, :width, :] = lax.dot_general(
            got, chosen, (((0,), (0,)), ((), ())), preferred_element_type=jnp.float32
        )

    moves = jnp.broadcast_to(ids[8:9, :], (8, LANES))
    bits = {b: (moves & b) != 0 for b in (128, 64, 32, 16, 8, 4, 2, 1)}

    def choose(bit, one, zero):
        return [jnp.where(bits[bit], p, q) for p, q in zip(one, zero)]

    def coarse(c, b):
        at = b * 64
        tiles = [xs[c, pl.ds(at + 8 * q, 8), :] for q in range(39)]
        for bit in (128, 64, 32, 16, 8):
            tiles = choose(bit, tiles[bit // 8 :], tiles[: -(bit // 8)])
        for q, tile in enumerate(tiles):
            ys[pl.ds(at + 8 * q, 8), :] = tile

    def fine(c, b):
        for q in range(5):
            at = b * 40 + 8 * q
            tiles = [ys[pl.ds(at + i, 8), :] for i in range(8)]
            for bit in (4, 2, 1):
                tiles = choose(bit, tiles[bit : 2 * bit], tiles[:bit])
            xt[c, pl.ds(at, 8), :] = tiles[0]

    def squares(c, at, count):
        total = None
        for i in range(count):
            x = xt[c, pl.ds(at + i, 8), :]
            total = x * x if total is None else total + x * x
        return total

    def eights(c, b):
        for q in range(4):
            at = b * 32 + 8 * q
            es[pl.ds(at, 8), :] = squares(c, at, 8)

    steps = taps // 8
    rest = taps - steps * 8

    def scales(c):
        run = [es[8 * q : 8 * q + 8, :] for q in range(OUT // 8 + steps - 1)]
        pieces = []
        size = 1
        while size <= steps:
            if steps & size:
                pieces.append((size, run))
            run = [p + q for p, q in zip(run, run[size:])]
            size *= 2
        for q in range(OUT // 8):
            done = 0
            total = squares(c, 8 * (q + steps), rest) if rest else None
            for size, piece in reversed(pieces):
                term = piece[q + done]
                total = term if total is None else total + term
                done += size
            it[c, 8 * q : 8 * q + 8, :] = lax.rsqrt(total / taps + 1e-05) * tinv[c]

    chan[...] = jnp.zeros_like(chan)
    tiles = 16

    def parts(c, b):
        for q in range(5):
            at = b * 40 + 8 * q
            x0 = xt[c, pl.ds(2 * at, 8, stride=2), :]
            x1 = xt[c, pl.ds(2 * at + 1, 8, stride=2), :]
            x2 = xt[c, pl.ds(2 * at + 2, 8, stride=2), :]
            xa[0, pl.ds(at, 8), :] = x1
            xa[1, pl.ds(at, 8), :] = x0 - x1
            xa[2, pl.ds(at, 8), :] = x2 - x1

    def correlate(c, m):
        def phase(count):
            def body(f, acc):
                win = [xa[m, pl.ds(f + 8 * q, 8), :] for q in range(tiles)]
                for e in range(count):
                    h = jnp.broadcast_to(ha[c, m, pl.ds(f + 8 * e, 1), :], (8, LANES))
                    acc = tuple(a + h * w for a, w in zip(acc, win))
                    if e < count - 1:
                        win = win[1:] + [xa[m, pl.ds(f + 8 * (tiles + e), 8), :]]
                return acc

            return body

        taken = taps // 2
        acc = tuple(jnp.zeros((8, LANES), jnp.float32) for _ in range(tiles))
        acc = lax.fori_loop(0, taken % 8, phase(taken // 8 + 1), acc)
        acc = lax.fori_loop(taken % 8, 8, phase(taken // 8), acc)
        for q in range(tiles):
            af[m, 8 * q : 8 * q + 8, :] = acc[q]

    def component(c):
        gather(c)
        each(0, 9, lambda b: coarse(c, b))
        each(0, 14, lambda b: fine(c, b))
        each(0, 17, lambda b: eights(c, b))
        scales(c)
        each(0, 7, lambda b: parts(c, b))
        each(0, 3, lambda m: correlate(c, m))
        for q in range(tiles):
            at = slice(8 * q, 8 * q + 8)
            common = af[0, at, :]
            even = it[c, pl.ds(16 * q, 8, stride=2), :]
            odd = it[c, pl.ds(16 * q + 1, 8, stride=2), :]
            chan[0, at, :] += (common + af[1, at, :]) * even
            chan[1, at, :] += (common + af[2, at, :]) * odd

    each(0, 3, component)
    for q in range(tiles):
        line[pl.ds(16 * q, 8, stride=2), :] = chan[0, 8 * q : 8 * q + 8, :]
        line[pl.ds(16 * q + 1, 8, stride=2), :] = chan[1, 8 * q : 8 * q + 8, :]
    flat = jnp.concatenate([line[v : v + LANES, :].T for v in range(0, OUT, LANES)], axis=1)
    stack = jnp.concatenate(
        [jnp.sum(flat[k * nstat : (k + 1) * nstat], axis=0, keepdims=True) for k in range(sets)],
        axis=0,
    )
    stack_ref[...] = stack
    best = jnp.max(stack, axis=0, keepdims=True)
    mine[...] = best
    each(1, n, lambda d: tell(d).start())
    held[me] = best
    each(1, n, lambda d: tell(d).wait_recv())
    peak_ref[...] = jnp.max(held[...], axis=0)
    for sent in (ask, functools.partial(give, 0), functools.partial(give, 1), tell):
        each(1, n, functools.partial(lambda copy, d: copy(d).wait_send(), sent))


def on_device(records, templates, fetch_list, cluster_slots, moveouts):
    n = fetch_list.shape[1]
    stations, comps, width = records.shape
    sets, nstat = cluster_slots.shape
    taps = templates.shape[-1]
    padded = -(-taps // LANES) * LANES
    used = -(-(OUT + taps - 1) // LANES)
    rec_flat = jnp.transpose(records, (1, 0, 2)).reshape(comps * stations, width)
    kernels = jnp.transpose(templates, (0, 2, 1, 3))
    vmem = pl.BlockSpec(memory_space=pltpu.VMEM)
    far = pl.BlockSpec(memory_space=pltpu.HBM)
    many = pltpu.SemaphoreType.DMA((2, n))
    sems = pltpu.SemaphoreType.DMA((n,))
    stack, peak = pl.pallas_call(
        functools.partial(kernel, n, stations, sets, nstat, taps),
        out_shape=(
            jax.ShapeDtypeStruct((sets, OUT), jnp.float32),
            jax.ShapeDtypeStruct((1, OUT), jnp.float32),
        ),
        in_specs=[far] * 5,
        out_specs=(vmem, vmem),
        scratch_shapes=[
            pltpu.SMEM((fetch_list.shape[2], n), jnp.int32),
            pltpu.VMEM(cluster_slots.shape, jnp.int32),
            pltpu.VMEM(moveouts.shape, jnp.int32),
            pltpu.VMEM(rec_flat.shape, jnp.bfloat16),
            pltpu.VMEM(kernels.shape, jnp.bfloat16),
            pltpu.VMEM((n, 1, LANES), jnp.int32),
            pltpu.VMEM((n, 1, LANES), jnp.int32),
            pltpu.VMEM((3, n, 2, width), jnp.bfloat16),
            pltpu.VMEM((3, n, 2, width), jnp.bfloat16),
            pltpu.VMEM((16, LANES), jnp.int32),
            pltpu.VMEM((3, 832, LANES), jnp.float32),
            pltpu.VMEM((576, LANES), jnp.float32),
            pltpu.VMEM((544, LANES), jnp.float32),
            pltpu.VMEM((3, used * LANES, LANES), jnp.float32),
            pltpu.VMEM((3, OUT, LANES), jnp.float32),
            pltpu.VMEM((3, LANES, padded), jnp.float32),
            pltpu.VMEM((3, padded, LANES), jnp.float32),
            pltpu.VMEM((3, 8, LANES), jnp.float32),
            pltpu.VMEM((3, 280, LANES), jnp.float32),
            pltpu.VMEM((3, 3, padded // 2, LANES), jnp.float32),
            pltpu.VMEM((3, OUT // 2, LANES), jnp.float32),
            pltpu.VMEM((OUT, LANES), jnp.float32),
            pltpu.VMEM((2, OUT // 2, LANES), jnp.float32),
            pltpu.VMEM((1, OUT), jnp.float32),
            pltpu.VMEM((n, 1, OUT), jnp.float32),
            pltpu.SemaphoreType.DMA((5,)),
            sems, sems, many, many, sems, sems,
        ],
        compiler_params=pltpu.CompilerParams(
            collective_id=0, has_side_effects=True, vmem_limit_bytes=60 << 20
        ),
        name="network_stack",
    )(jnp.transpose(fetch_list[0]), cluster_slots, moveouts, rec_flat, kernels)
    return stack, peak.reshape(OUT)


def solution(mesh):
    placed = (
        P(("groups", "tmpl"), None, None),
        P("tmpl", None, None, None),
        P("tmpl", None, None),
        P("tmpl", None),
        P("tmpl", None),
    )
    return jax.shard_map(
        on_device,
        mesh=mesh,
        in_specs=placed,
        out_specs=(P(("groups", "tmpl"), None), P("groups")),
        check_vma=False,
    )
```
